32 devices in a mesh: depth: 4 (over z), tile: 8 (over y, x, core).
Axes of the slice: x: 2, y: 2, z: 4, core: 2. Of those that a mesh axis runs over, the one named last changes fastest.
Arguments:
- amplitude: float32 [8, 8, 256, 256], P('depth', 'tile'), may hold values from 0.7 to 1.3
- phase_map: float32 [8, 8, 256, 256], P('depth', 'tile'), may hold values from -3.140625 to 3.140625
- probe_wave: float32 [2, 128, 128], replicated, may hold values from -4 to 4
- propagator_phase: float32 [2, 128], replicated, may hold values from -3.140625 to 3.140625
- positions: int32 [8, 4, 2], P('tile'), may hold values from -64 to 192
- measured: float32 [8, 4, 128, 128], P('tile'), may hold values from 0 to 1
Outputs:
- object_gradient: float32 [2, 8, 8, 256, 256], P(None, 'depth', 'tile')
The draws below stay inside these ranges and needn't reach their ends.
Inputs may be any that keep to these rules, and one draw needn't show every extreme that they name: `positions`: every window of 128 x 128 pixels starting at a position lies within 64 pixels of its tile.
All inputs are finite; a program needn't handle non-finite values.
Results may differ from the reference program's by a relative error of at most 0.02.
Values may be sent and summed in bfloat16 or wider, within the bound.
A program may use at most 128 MiB of HBM per device.

```python
import math
import jax
import jax.numpy as jnp
from jax import lax

PROBE = 128
RIM = 64
SLICE_DEV = 2
TILE = 256
WAVES = 4
SLICES = 8
TILES = 8
TCOLS = 2


def plant(values, key, least, high):
    spot = [jax.random.randint(jax.random.fold_in(key, axis), (), 0, length) for axis, length in enumerate(values.shape)]
    main_axis = values.shape.index(max(values.shape))
    next_to = spot[:main_axis] + [(spot[main_axis] + 1) % values.shape[main_axis]] + spot[main_axis + 1:]
    return values.at[tuple(spot)].set(least).at[tuple(next_to)].set(high)


def block_scale(rng, extent, cuts, smallest, largest):
    loudness, own = 1.0, jax.random.fold_in(rng, 6)
    for axis_at, blocks in cuts:
        draws = jnp.exp(jax.random.uniform(jax.random.fold_in(own, axis_at), (blocks,), jnp.float32, smallest / len(cuts), largest / len(cuts)))
        loudness = loudness * jnp.repeat(draws, extent[axis_at] // blocks).reshape([-1 if axis == axis_at else 1 for axis in range(len(extent))])
    return loudness


def scatter_about(own_key, shape, scale, reach, held_as=jnp.bfloat16):
    return jnp.clip(scale * jax.random.normal(own_key, shape, jnp.float32), -reach, reach).astype(held_as)


def setup_inputs(seed: int = 0) -> dict:
    keys = jax.random.split(jax.random.key(seed), 7)
    amplitude = jnp.clip(jnp.exp(math.log(1.3) - 0.6190392 * jax.random.uniform(keys[0], (SLICES, TILES, TILE, TILE), jnp.float32) ** block_scale(keys[0], (SLICES, TILES, TILE, TILE), ((0, 4), (1, 8)), -0.2, 0.2)), 0.7, 1.3)
    phase_map = jnp.clip(jax.random.uniform(keys[1], (SLICES, TILES, TILE, TILE), jnp.float32, -3.140625, 3.140625), -3.140625, 3.140625)
    probe_wave = scatter_about(keys[2], (2, PROBE, PROBE), 0.5, 4.0, jnp.float32)
    propagator_phase = jnp.clip(jax.random.uniform(keys[3], (2, PROBE), jnp.float32, -3.140625, 3.140625), -3.140625, 3.140625)
    positions = plant(jax.random.randint(keys[4], (TILES, WAVES, 2), -RIM, TILE + RIM - PROBE + 1), jax.random.fold_in(keys[4], 1), -RIM, TILE + RIM - PROBE).astype(jnp.int32)
    measured = jnp.clip(1.0 * jax.random.uniform(keys[5], (TILES, WAVES, PROBE, PROBE), jnp.float32) ** block_scale(keys[5], (TILES, WAVES, PROBE, PROBE), ((0, 8),), -0.2, 0.2), 0.0, 1.0)
    return dict(amplitude=amplitude, phase_map=phase_map, probe_wave=probe_wave, propagator_phase=propagator_phase, positions=positions, measured=measured)


PRECISE = lax.Precision.HIGHEST

def dft_tables(points):
    points_line = jnp.arange(points, dtype=jnp.int32)
    products = points_line[:, None] * points_line[None, :] % points
    angles = products.astype(jnp.float32) * (-2.0 * math.pi / points)
    norm_factor = 1.0 / math.sqrt(points)
    return (jnp.cos(angles) * norm_factor, jnp.sin(angles) * norm_factor)

def left_product(mat_real, mat_imag, wave_real, wave_imag):

    def multiply(matrix, operand):
        return jnp.einsum('ij,...jk->...ik', matrix, operand, precision=PRECISE)
    return (multiply(mat_real, wave_real) - multiply(mat_imag, wave_imag), multiply(mat_real, wave_imag) + multiply(mat_imag, wave_real))

def right_product(wave_real, wave_imag, mat_real, mat_imag):

    def multiply(operand, matrix):
        return jnp.einsum('...ij,jk->...ik', operand, matrix, precision=PRECISE)
    return (multiply(wave_real, mat_real) - multiply(wave_imag, mat_imag), multiply(wave_imag, mat_real) + multiply(wave_real, mat_imag))

def build_operators(propagator_phase, tables):
    dft_real, dft_imag = tables
    result = []
    for axis_row in range(2):
        cosine = jnp.cos(propagator_phase[axis_row])[:, None]
        sine_part = jnp.sin(propagator_phase[axis_row])[:, None]
        scaled_real = cosine * dft_real - sine_part * dft_imag
        scaled_imag = cosine * dft_imag + sine_part * dft_real
        result.extend(left_product(dft_real, -dft_imag, scaled_real, scaled_imag))
    return tuple(result)

def to_wire(values):
    return lax.optimization_barrier(values.astype(jnp.bfloat16)).astype(jnp.float32)

def forward_pass(waves, patch_real, patch_imag, operators, group_size):
    row_real, row_imag, col_real, col_imag = operators
    wave_real, wave_imag = (waves[0], waves[1])
    slice_count = patch_real.shape[1]
    kept_real, kept_imag = ([], [])
    for layer_number in range(slice_count):
        kept_real.append(wave_real)
        kept_imag.append(wave_imag)
        slab_real = patch_real[:, layer_number]
        slab_imag = patch_imag[:, layer_number]
        mixed_real = slab_real * wave_real - slab_imag * wave_imag
        mixed_imag = slab_real * wave_imag + slab_imag * wave_real
        half_real, half_imag = left_product(row_real, row_imag, mixed_real, mixed_imag)
        wave_real, wave_imag = right_product(half_real, half_imag, col_real.T, col_imag.T)
        if (layer_number + 1) % group_size == 0 and layer_number + 1 < slice_count:
            wave_real = to_wire(wave_real)
            wave_imag = to_wire(wave_imag)
    return (jnp.stack([wave_real, wave_imag]), jnp.stack(kept_real, axis=1), jnp.stack(kept_imag, axis=1))

def adjoint_pass(backflow, kept_real, kept_imag, patch_real, patch_imag, operators, group_size):
    row_real, row_imag, col_real, col_imag = operators
    back_real, back_imag = (backflow[0], backflow[1])
    slice_count = patch_real.shape[1]
    grads_real = [None] * slice_count
    grads_imag = [None] * slice_count
    for layer_number in reversed(range(slice_count)):
        half_real, half_imag = left_product(row_real.T, -row_imag.T, back_real, back_imag)
        spread_real, spread_imag = right_product(half_real, half_imag, col_real, -col_imag)
        input_real = kept_real[:, layer_number]
        input_imag = kept_imag[:, layer_number]
        grads_real[layer_number] = input_real * spread_real + input_imag * spread_imag
        grads_imag[layer_number] = input_real * spread_imag - input_imag * spread_real
        slab_real = patch_real[:, layer_number]
        slab_imag = patch_imag[:, layer_number]
        back_real = slab_real * spread_real + slab_imag * spread_imag
        back_imag = slab_real * spread_imag - slab_imag * spread_real
        if layer_number % group_size == 0 and layer_number > 0:
            back_real = to_wire(back_real)
            back_imag = to_wire(back_imag)
    return (jnp.stack([back_real, back_imag]), jnp.stack(grads_real, axis=1), jnp.stack(grads_imag, axis=1))

def farfield_residual(waves, observed, tables):
    dft_real, dft_imag = tables
    half_real, half_imag = left_product(dft_real, dft_imag, waves[0], waves[1])
    far_real, far_imag = right_product(half_real, half_imag, dft_real, dft_imag)
    misfit = far_real * far_real + far_imag * far_imag - observed
    inverse_real, inverse_imag = left_product(dft_real, -dft_imag, misfit * far_real, misfit * far_imag)
    back_real, back_imag = right_product(inverse_real, inverse_imag, dft_real, -dft_imag)
    return jnp.stack([back_real, back_imag])

def cut_patches(transmission, windows, points):

    def one_window(window):
        anchor = (jnp.int32(0), jnp.int32(0), window[0], window[1])
        return lax.dynamic_slice(transmission, anchor, (2, transmission.shape[1], points, points))
    patches = jax.vmap(one_window)(windows)
    return (patches[:, 0], patches[:, 1])

def deposit(buffer, grad_real, grad_imag, windows):
    points = grad_real.shape[-1]

    def add_one(number, current):
        window = windows[number]
        anchor = (jnp.int32(0), jnp.int32(0), window[0], window[1])
        previous = lax.dynamic_slice(current, anchor, (2, current.shape[1], points, points))
        fresh = previous + jnp.stack([grad_real[number], grad_imag[number]])
        return lax.dynamic_update_slice(current, fresh, anchor)
    return lax.fori_loop(0, windows.shape[0], add_one, buffer)

def reference(amplitude, phase_map, probe_wave, propagator_phase, positions, measured):
    slice_count = amplitude.shape[0]
    tile_count = amplitude.shape[1]
    tile_size = amplitude.shape[-1]
    grid_rows = tile_count // TCOLS

    def assemble(values):
        shaped = values.reshape(slice_count, grid_rows, TCOLS, tile_size, tile_size)
        shaped = jnp.transpose(shaped, (0, 1, 3, 2, 4))
        return shaped.reshape(slice_count, grid_rows * tile_size, TCOLS * tile_size)

    def split_back(values):
        shaped = values.reshape(2, slice_count, grid_rows, tile_size, TCOLS, tile_size)
        shaped = jnp.transpose(shaped, (0, 1, 2, 4, 3, 5))
        return shaped.reshape(2, slice_count, tile_count, tile_size, tile_size)
    amplitude_full = assemble(amplitude)
    phase_full = assemble(phase_map)
    transmission = jnp.stack([amplitude_full * jnp.cos(phase_full), amplitude_full * jnp.sin(phase_full)])
    transmission = jnp.pad(transmission, ((0, 0), (0, 0), (RIM, RIM), (RIM, RIM)))
    tables = dft_tables(PROBE)
    operators = build_operators(propagator_phase, tables)
    starting = jnp.broadcast_to(probe_wave[:, None], (2, WAVES, PROBE, PROBE))

    def one_tile(buffer, inputs):
        tile_number, corners, observed = inputs
        corner = jnp.stack([tile_number // TCOLS * tile_size, tile_number % TCOLS * tile_size]).astype(jnp.int32)
        windows = (corners + corner[None, :] + RIM).astype(jnp.int32)
        patch_real, patch_imag = cut_patches(transmission, windows, PROBE)
        exit_wave, kept_real, kept_imag = forward_pass(starting, patch_real, patch_imag, operators, SLICE_DEV)
        backflow = farfield_residual(exit_wave, observed, tables)
        unused, grad_real, grad_imag = adjoint_pass(backflow, kept_real, kept_imag, patch_real, patch_imag, operators, SLICE_DEV)
        return (deposit(buffer, grad_real, grad_imag, windows), None)
    buffer = jnp.zeros(transmission.shape, jnp.float32)
    buffer, unused = lax.scan(one_tile, buffer, (jnp.arange(tile_count, dtype=jnp.int32), positions, measured))
    height = grid_rows * tile_size
    full_width = TCOLS * tile_size
    return split_back(buffer[:, :, RIM:RIM + height, RIM:RIM + full_width])
```

```python
import functools
import math

import jax
import jax.numpy as jnp
import numpy as np
from jax import lax
from jax.experimental import pallas as pl
from jax.experimental.pallas import tpu as pltpu
from jax.sharding import PartitionSpec as P

RIM = 64
LANES = 128
MESH = pl.DeviceIdType.MESH
F32 = jnp.float32
BF16 = jnp.bfloat16
DIRECTIONS = tuple((dr, dc) for dr in (-1, 0, 1) for dc in (-1, 0, 1) if (dr, dc) != (0, 0))


def dft_constants(points):
    line = np.arange(points)
    angles = (line[:, None] * line[None, :] % points) * (-2.0 * math.pi / points)
    real = np.cos(angles) / math.sqrt(points)
    imag = np.sin(angles) / math.sqrt(points)
    left = np.block([[real, -imag], [imag, real]])
    right = np.block([[real, imag], [-imag, real]])
    both = np.stack([left, right]).astype(np.float32)
    high = both.astype(BF16)
    low = (both - high.astype(np.float32)).astype(BF16)
    return np.stack([high, low], axis=1)


def cos_sin(angle):
    half = angle * 0.5
    square = half * half
    sine = F32((1.0 / 6227020800.0))
    for term in (-1 / 39916800.0, 1 / 362880.0, -1 / 5040.0, 1 / 120.0, -1 / 6.0, 1.0):
        sine = sine * square + F32(term)
    sine = sine * half
    cosine = F32(1 / 479001600.0)
    for term in (-1 / 3628800.0, 1 / 40320.0, -1 / 720.0, 1 / 24.0, -0.5, 1.0):
        cosine = cosine * square + F32(term)
    return 1.0 - 2.0 * sine * sine, 2.0 * sine * cosine


def dot(a, b):
    return jnp.dot(a, b, preferred_element_type=F32)


def split(value):
    high = value.astype(BF16)
    return high, (value - high.astype(F32)).astype(BF16)


def right_product(real, imag, high, low):
    points = real.shape[-1]
    x_high, x_low = split(jnp.concatenate([real, imag], axis=1))
    result = dot(x_high, high) + (dot(x_low, high) + dot(x_high, low))
    return result[:, :points], result[:, points:]


def left_product(high, low, real, imag):
    points = real.shape[0]
    v_high, v_low = split(jnp.concatenate([real, imag], axis=0))
    both = dot(high, jnp.concatenate([v_high, v_low], axis=1))
    result = both[:, :points] + (both[:, points:] + dot(low, v_high))
    return result[:points], result[points:]


def kernel(
    depth_count,
    tile_count,
    columns,
    pos_ref,
    amp_ref,
    phase_ref,
    probe_ref,
    prop_ref,
    meas_ref,
    dft_ref,
    out_ref,
    ext,
    cut_row,
    cut_col,
    put_row,
    put_col,
    mats,
    psend,
    pat,
    kept,
    back,
    csend,
    cin,
    grad,
    *rest,
):
    rim_send, rim_recv = rest[:8], rest[8:16]
    halo_s, halo_r, pat_s, pat_r, con_s, con_r, fold_s, fold_r = rest[16:]
    group, size = amp_ref.shape[0], amp_ref.shape[-1]
    waves, points = meas_ref.shape[0], meas_ref.shape[-1]
    slices = group * depth_count
    height = size + 2 * RIM
    width = size + 2 * LANES
    rows = tile_count // columns
    d = lax.axis_index("depth")
    t = lax.axis_index("tile")
    row, col = t // columns, t % columns

    def exists(dr, dc):
        return (row + dr >= 0) & (row + dr < rows) & (col + dc >= 0) & (col + dc < columns)

    def neighbour(dr, dc):
        return {"depth": d, "tile": t + dr * columns + dc}

    barrier = pltpu.get_barrier_semaphore()
    mates = [lax.rem(d + k, depth_count) for k in range(1, depth_count)]
    for mate in mates:
        pl.semaphore_signal(barrier, inc=1, device_id={"depth": mate, "tile": t}, device_id_type=MESH)
    for dr, dc in DIRECTIONS:

        @pl.when(exists(dr, dc))
        def _():
            pl.semaphore_signal(barrier, inc=1, device_id=neighbour(dr, dc), device_id_type=MESH)

    rows_in = {-1: (0, RIM), 0: (RIM, size), 1: (RIM + size, RIM)}
    cols_in = {-1: (0, LANES), 0: (LANES, size), 1: (LANES + size, LANES)}
    rows_own = {-1: (RIM, RIM), 0: (RIM, size), 1: (size, RIM)}
    cols_own = {-1: (LANES, LANES), 0: (LANES, size), 1: (size, LANES)}

    def halo_copy(i, k):
        dr, dc = DIRECTIONS[k]
        back_k = DIRECTIONS.index((-dr, -dc))
        return pltpu.make_async_remote_copy(
            src_ref=ext.at[i, :, pl.ds(*rows_own[dr]), pl.ds(*cols_own[dc])],
            dst_ref=ext.at[i, :, pl.ds(*rows_in[-dr]), pl.ds(*cols_in[-dc])],
            send_sem=halo_s.at[i, k],
            recv_sem=halo_r.at[i, back_k],
            device_id=neighbour(dr, dc),
            device_id_type=MESH,
        )

    def halo_arrival(i, k):
        dr, dc = DIRECTIONS[k]
        region = ext.at[i, :, pl.ds(*rows_in[dr]), pl.ds(*cols_in[dc])]
        return pltpu.make_async_remote_copy(
            src_ref=region,
            dst_ref=region,
            send_sem=halo_s.at[i, k],
            recv_sem=halo_r.at[i, k],
            device_id=neighbour(dr, dc),
            device_id_type=MESH,
        )

    for i in range(group):
        cosine, sine = cos_sin(phase_ref[i, 0])
        ext[i, 0, RIM : RIM + size, LANES : LANES + size] = (amp_ref[i, 0] * cosine).astype(BF16)
        ext[i, 1, RIM : RIM + size, LANES : LANES + size] = (amp_ref[i, 0] * sine).astype(BF16)
        if i == 0:
            peers = depth_count - 1
            for dr, dc in DIRECTIONS:
                peers += exists(dr, dc).astype(jnp.int32)
            pl.semaphore_wait(barrier, peers)

        for k, (dr, dc) in enumerate(DIRECTIONS):

            @pl.when(exists(dr, dc))
            def _():
                halo_copy(i, k).start()

            @pl.when(jnp.logical_not(exists(dr, dc)))
            def _():
                r0, rn = rows_in[dr]
                c0, cn = cols_in[dc]
                ext[i, :, r0 : r0 + rn, c0 : c0 + cn] = jnp.zeros((2, rn, cn), BF16)

    def one_hot(shape, shifted_axis, shift):
        along = lax.broadcasted_iota(jnp.int32, shape, shifted_axis)
        other = lax.broadcasted_iota(jnp.int32, shape, 1 - shifted_axis)
        return jnp.where(along == other + shift, F32(1), F32(0)).astype(BF16)

    for w in range(waves):
        r = pos_ref[0, 0, w] + RIM
        c = pos_ref[0, 1, w] + LANES
        span = slice(w * points, (w + 1) * points)
        cut_row[span, :] = one_hot((points, height), 1, r)
        cut_col[w] = one_hot((width, points), 0, c)
        put_row[:, span] = one_hot((height, points), 0, r)
        put_col[w] = one_hot((points, width), 1, c)

    f_left_h, f_left_l = dft_ref[0, 0], dft_ref[0, 1]
    f_right_h, f_right_l = dft_ref[1, 0], dft_ref[1, 1]
    f_full = f_right_h.astype(F32) + f_right_l.astype(F32)
    f_real, f_imag = f_full[:points, :points], f_full[:points, points:]

    def propagator(axis, sign):
        cosine, sine = cos_sin(prop_ref[axis : axis + 1, :])
        sine = sine * sign
        a_real = f_real * cosine + f_imag * sine
        a_imag = f_real * sine - f_imag * cosine
        return right_product(a_real, a_imag, f_right_h, f_right_l)

    def keep(n, top_right, bottom_left, real):
        high, low = split(
            jnp.concatenate(
                [
                    jnp.concatenate([real, top_right], axis=1),
                    jnp.concatenate([bottom_left, real], axis=1),
                ],
                axis=0,
            )
        )
        mats[n, 0] = high
        mats[n, 1] = low

    real, imag = propagator(0, 1.0)
    keep(0, -imag, imag, real)
    real, imag = propagator(1, -1.0)
    keep(1, -imag, imag, real)
    real, imag = propagator(0, -1.0)
    keep(2, -imag, imag, real)
    real, imag = propagator(1, 1.0)
    keep(3, -imag, imag, real)

    def patch_copy(i, k):
        mate = mates[k]
        return pltpu.make_async_remote_copy(
            src_ref=psend.at[mate, i],
            dst_ref=pat.at[d * group + i],
            send_sem=pat_s.at[i, k],
            recv_sem=pat_r.at[d * group + i],
            device_id={"depth": mate, "tile": t},
            device_id_type=MESH,
        )

    for i in range(group):
        for k, (dr, dc) in enumerate(DIRECTIONS):

            @pl.when(exists(dr, dc))
            def _():
                halo_arrival(i, k).wait_recv()

        bands = [dot(cut_row[...], ext[i, c]).astype(BF16) for c in range(2)]
        for w in range(waves):
            span = slice(w * points, (w + 1) * points)
            both = jnp.concatenate([bands[0][span], bands[1][span]], axis=0)
            cut = dot(both, cut_col[w]).astype(BF16)
            psend[w, i, 0] = cut[:points]
            psend[w, i, 1] = cut[points:]
        for k in range(depth_count - 1):
            patch_copy(i, k).start()
        pat[d * group + i] = psend[d, i]

    def await_patch(s):
        @pl.when(s // group != d)
        def _():
            pltpu.make_async_remote_copy(
                src_ref=pat.at[s],
                dst_ref=pat.at[s],
                send_sem=pat_s.at[0, 0],
                recv_sem=pat_r.at[s],
                device_id={"depth": mates[0], "tile": t},
                device_id_type=MESH,
            ).wait_recv()

    def mixed(s):
        p_real, p_imag = pat[s, 0].astype(F32), pat[s, 1].astype(F32)
        w_real, w_imag = kept[s, 0], kept[s, 1]
        return p_real * w_real - p_imag * w_imag, p_real * w_imag + p_imag * w_real

    kept[0] = probe_ref[...]

    def forward(s, carry):
        await_patch(s)
        real, imag = mixed(s)
        real, imag = right_product(real, imag, mats[1, 0], mats[1, 1])
        real, imag = left_product(mats[0, 0], mats[0, 1], real, imag)
        kept[s + 1, 0] = real
        kept[s + 1, 1] = imag
        return carry

    lax.fori_loop(0, slices - 1, forward, 0)
    last = slices - 1
    await_patch(last)

    def contribution_copy(s):
        return pltpu.make_async_remote_copy(
            src_ref=csend.at[s],
            dst_ref=cin.at[s % group, d],
            send_sem=con_s.at[s],
            recv_sem=con_r.at[s % group, d],
            device_id={"depth": s // group, "tile": t},
            device_id_type=MESH,
        )

    def contribute(s, s_real, s_imag):
        w_real, w_imag = kept[s, 0], kept[s, 1]
        csend[s, 0] = (w_real * s_real + w_imag * s_imag).astype(BF16)
        csend[s, 1] = (w_real * s_imag - w_imag * s_real).astype(BF16)

        @pl.when(s // group != d)
        def _():
            contribution_copy(s).start()

        @pl.when(s // group == d)
        def _():
            cin[s % group, d] = csend[s]

        p_real, p_imag = pat[s, 0].astype(F32), pat[s, 1].astype(F32)
        back[0] = p_real * s_real + p_imag * s_imag
        back[1] = p_real * s_imag - p_imag * s_real

    real, imag = mixed(last)
    real, imag = right_product(real, imag, f_right_h, f_right_l)
    real, imag = left_product(f_left_h, f_left_l, real, imag)
    misfit = real * real + imag * imag - meas_ref[d]
    real, imag = right_product(misfit * real, misfit * imag, f_left_h, f_left_l)
    real, imag = left_product(f_right_h, f_right_l, real, imag)
    contribute(last, real, imag)

    def backward(number, carry):
        s = last - 1 - number
        real, imag = right_product(back[0], back[1], mats[3, 0], mats[3, 1])
        real, imag = left_product(mats[2, 0], mats[2, 1], real, imag)
        contribute(s, real, imag)
        return carry

    lax.fori_loop(0, slices - 1, backward, 0)

    def fold_copy(i, k):
        dr, dc = DIRECTIONS[k]
        back_k = DIRECTIONS.index((-dr, -dc))
        return pltpu.make_async_remote_copy(
            src_ref=rim_send[k].at[i],
            dst_ref=rim_recv[back_k].at[i],
            send_sem=fold_s.at[i, k],
            recv_sem=fold_r.at[i, back_k],
            device_id=neighbour(dr, dc),
            device_id_type=MESH,
        )

    def fold_arrival(i, k):
        dr, dc = DIRECTIONS[k]
        return pltpu.make_async_remote_copy(
            src_ref=rim_recv[k].at[i],
            dst_ref=rim_recv[k].at[i],
            send_sem=fold_s.at[i, k],
            recv_sem=fold_r.at[i, k],
            device_id=neighbour(dr, dc),
            device_id_type=MESH,
        )

    for i in reversed(range(group)):
        for w in range(waves):

            @pl.when(d != w)
            def _():
                pltpu.make_async_remote_copy(
                    src_ref=cin.at[i, w],
                    dst_ref=cin.at[i, w],
                    send_sem=con_s.at[0],
                    recv_sem=con_r.at[i, w],
                    device_id={"depth": mates[0], "tile": t},
                    device_id_type=MESH,
                ).wait_recv()

        for c in range(2):
            spread = [dot(cin[i, w, c], put_col[w]).astype(BF16) for w in range(waves)]
            grad[c] = dot(put_row[...], jnp.concatenate(spread, axis=0))
            out_ref[c, i, 0] = grad[c, RIM : RIM + size, LANES : LANES + size]
            for k, (dr, dc) in enumerate(DIRECTIONS):
                r0, rn = rows_in[dr]
                c0, cn = cols_in[dc]
                rim_send[k][i, c] = grad[c, r0 : r0 + rn, c0 : c0 + cn].astype(BF16)
        for k, (dr, dc) in enumerate(DIRECTIONS):

            @pl.when(exists(dr, dc))
            def _():
                fold_copy(i, k).start()

    add_row = {-1: 0, 0: 0, 1: size - RIM}
    add_col = {-1: 0, 0: 0, 1: size - LANES}
    for i in reversed(range(group)):
        for k, (dr, dc) in enumerate(DIRECTIONS):

            @pl.when(exists(dr, dc))
            def _():
                fold_arrival(i, k).wait_recv()
                r0, rn = add_row[dr], rows_in[dr][1]
                c0, cn = add_col[dc], cols_in[dc][1]
                for c in range(2):
                    out_ref[c, i, 0, r0 : r0 + rn, c0 : c0 + cn] += rim_recv[k][i, c].astype(F32)

    for i in range(group):
        for k in range(depth_count - 1):
            patch_copy(i, k).wait_send()
        for k, (dr, dc) in enumerate(DIRECTIONS):

            @pl.when(exists(dr, dc))
            def _():
                halo_copy(i, k).wait_send()
                fold_copy(i, k).wait_send()

    for s in range(slices):

        @pl.when(d != s // group)
        def _():
            contribution_copy(s).wait_send()


def shards(depth_count, tile_count, amplitude, phase_map, probe_wave, propagator_phase, positions, measured):
    columns = max(2, tile_count // 8)
    group, size = amplitude.shape[0], amplitude.shape[-1]
    points = probe_wave.shape[-1]
    waves = positions.shape[1]
    slices = group * depth_count
    assert waves == depth_count
    height, width = size + 2 * RIM, size + 2 * LANES
    rims = []
    for dr, dc in DIRECTIONS:
        shape = (group, 2, RIM if dr else size, LANES if dc else size)
        rims.append(pltpu.VMEM(shape, BF16))
    dma = pltpu.SemaphoreType.DMA
    vmem = pl.BlockSpec(memory_space=pltpu.VMEM)
    return pl.pallas_call(
        functools.partial(kernel, depth_count, tile_count, columns),
        out_shape=jax.ShapeDtypeStruct((2, group, 1, size, size), F32),
        in_specs=[pl.BlockSpec(memory_space=pltpu.SMEM)] + [vmem] * 6,
        out_specs=vmem,
        scratch_shapes=[
            pltpu.VMEM((group, 2, height, width), BF16),
            pltpu.VMEM((waves * points, height), BF16),
            pltpu.VMEM((waves, width, points), BF16),
            pltpu.VMEM((height, waves * points), BF16),
            pltpu.VMEM((waves, points, width), BF16),
            pltpu.VMEM((4, 2, 2 * points, 2 * points), BF16),
            pltpu.VMEM((waves, group, 2, points, points), BF16),
            pltpu.VMEM((slices, 2, points, points), BF16),
            pltpu.VMEM((slices, 2, points, points), F32),
            pltpu.VMEM((2, points, points), F32),
            pltpu.VMEM((slices, 2, points, points), BF16),
            pltpu.VMEM((group, waves, 2, points, points), BF16),
            pltpu.VMEM((2, height, width), F32),
            *rims,
            *rims,
            dma((group, 8)),
            dma((group, 8)),
            dma((group, depth_count)),
            dma((slices,)),
            dma((slices,)),
            dma((group, waves)),
            dma((group, 8)),
            dma((group, 8)),
        ],
        compiler_params=pltpu.CompilerParams(collective_id=0, has_side_effects=True),
    )(
        jnp.transpose(positions, (0, 2, 1)),
        amplitude,
        phase_map,
        probe_wave,
        propagator_phase,
        measured[0],
        jnp.asarray(dft_constants(points)),
    )


def solution(mesh):
    in_specs = (
        P("depth", "tile", None, None),
        P("depth", "tile", None, None),
        P(),
        P(),
        P("tile", None, None),
        P("tile", None, None, None),
    )
    out_specs = P(None, "depth", "tile", None, None)
    body = functools.partial(shards, mesh.shape["depth"], mesh.shape["tile"])
    return jax.shard_map(body, mesh=mesh, in_specs=in_specs, out_specs=out_specs, check_vma=False)
```

```python
import functools
import math

import jax
import jax.numpy as jnp
import numpy as np
from jax import lax
from jax.experimental import pallas as pl
from jax.experimental.pallas import tpu as pltpu
from jax.sharding import PartitionSpec as P

RIM = 64
LANES = 128
MESH = pl.DeviceIdType.MESH
F32 = jnp.float32
BF16 = jnp.bfloat16
SIDES = ((0, -1), (0, 1), (-1, 0), (1, 0))
DIRECTIONS = ((-1, 0), (1, 0), (0, -1), (0, 1)) + tuple((dr, dc) for dr in (-1, 1) for dc in (-1, 1))


def dft_constants(points):
    line = np.arange(points)
    angles = (line[:, None] * line[None, :] % points) * (-2.0 * math.pi / points)
    real = np.cos(angles) / math.sqrt(points)
    imag = np.sin(angles) / math.sqrt(points)
    left = np.block([[real, -imag], [imag, real]])
    right = np.block([[real, imag], [-imag, real]])
    both = np.stack([left, right]).astype(np.float32)
    high = both.astype(BF16)
    low = (both - high.astype(np.float32)).astype(BF16)
    return np.stack([high, low], axis=1)


def cos_sin(angle):
    half = angle * 0.5
    square = half * half
    sine = F32((1.0 / 6227020800.0))
    for term in (-1 / 39916800.0, 1 / 362880.0, -1 / 5040.0, 1 / 120.0, -1 / 6.0, 1.0):
        sine = sine * square + F32(term)
    sine = sine * half
    cosine = F32(1 / 479001600.0)
    for term in (-1 / 3628800.0, 1 / 40320.0, -1 / 720.0, 1 / 24.0, -0.5, 1.0):
        cosine = cosine * square + F32(term)
    return 1.0 - 2.0 * sine * sine, 2.0 * sine * cosine


def dot(a, b):
    return jnp.dot(a, b, preferred_element_type=F32)


def split(value):
    high = value.astype(BF16)
    return high, (value - high.astype(F32)).astype(BF16)


def right_product(real, imag, high, low):
    points = real.shape[-1]
    x_high, x_low = split(jnp.concatenate([real, imag], axis=1))
    result = dot(x_high, high) + (dot(x_low, high) + dot(x_high, low))
    return result[:, :points], result[:, points:]


def left_product(high, low, real, imag):
    points = real.shape[0]
    v_high, v_low = split(jnp.concatenate([real, imag], axis=0))
    both = dot(high, jnp.concatenate([v_high, v_low], axis=1))
    result = both[:, :points] + (both[:, points:] + dot(low, v_high))
    return result[:points], result[points:]


def kernel(
    depth_count,
    tile_count,
    columns,
    pos_ref,
    amp_ref,
    phase_ref,
    probe_ref,
    prop_ref,
    meas_ref,
    dft_ref,
    out_ref,
    ext,
    cut_row,
    cut_col,
    put_row,
    put_col,
    mats,
    psend,
    pat,
    kept,
    back,
    csend,
    cin,
    grad,
    *rest,
):
    rim_send, rim_recv = rest[:4], rest[4:8]
    halo_s, halo_r, pat_s, pat_r, con_s, con_r, fold_s, fold_r = rest[8:]
    group, size = amp_ref.shape[0], amp_ref.shape[-1]
    waves, points = meas_ref.shape[0], meas_ref.shape[-1]
    slices = group * depth_count
    height = size + 2 * RIM
    width = size + 2 * LANES
    rows = tile_count // columns
    d = lax.axis_index("depth")
    t = lax.axis_index("tile")
    row, col = t // columns, t % columns

    def exists(dr, dc):
        return (row + dr >= 0) & (row + dr < rows) & (col + dc >= 0) & (col + dc < columns)

    def neighbour(dr, dc):
        return {"depth": d, "tile": t + dr * columns + dc}

    barrier = pltpu.get_barrier_semaphore()
    mates = [lax.rem(d + k, depth_count) for k in range(1, depth_count)]
    for mate in mates:
        pl.semaphore_signal(barrier, inc=1, device_id={"depth": mate, "tile": t}, device_id_type=MESH)
    for dr, dc in DIRECTIONS:

        @pl.when(exists(dr, dc))
        def _():
            pl.semaphore_signal(barrier, inc=1, device_id=neighbour(dr, dc), device_id_type=MESH)

    rows_in = {-1: (0, RIM), 0: (RIM, size), 1: (RIM + size, RIM)}
    cols_in = {-1: (0, LANES), 0: (LANES, size), 1: (LANES + size, LANES)}
    rows_own = {-1: (RIM, RIM), 0: (RIM, size), 1: (size, RIM)}
    cols_own = {-1: (LANES, LANES), 0: (LANES, size), 1: (size, LANES)}

    def halo_copy(i, k):
        dr, dc = DIRECTIONS[k]
        corner = dr != 0 and dc != 0
        far_row = dr if corner else -dr
        back_k = DIRECTIONS.index((far_row, -dc))
        return pltpu.make_async_remote_copy(
            src_ref=ext.at[i, :, pl.ds(*(rows_in if corner else rows_own)[dr]), pl.ds(*cols_own[dc])],
            dst_ref=ext.at[i, :, pl.ds(*rows_in[far_row]), pl.ds(*cols_in[-dc])],
            send_sem=halo_s.at[i, k],
            recv_sem=halo_r.at[i, back_k],
            device_id=neighbour(0 if corner else dr, dc),
            device_id_type=MESH,
        )

    def halo_arrival(i, k):
        dr, dc = DIRECTIONS[k]
        region = ext.at[i, :, pl.ds(*rows_in[dr]), pl.ds(*cols_in[dc])]
        return pltpu.make_async_remote_copy(
            src_ref=region,
            dst_ref=region,
            send_sem=halo_s.at[i, k],
            recv_sem=halo_r.at[i, k],
            device_id=neighbour(dr, dc),
            device_id_type=MESH,
        )

    for i in range(group):
        cosine, sine = cos_sin(phase_ref[i, 0])
        ext[i, 0, RIM : RIM + size, LANES : LANES + size] = (amp_ref[i, 0] * cosine).astype(BF16)
        ext[i, 1, RIM : RIM + size, LANES : LANES + size] = (amp_ref[i, 0] * sine).astype(BF16)
        if i == 0:
            peers = depth_count - 1
            for dr, dc in DIRECTIONS:
                peers += exists(dr, dc).astype(jnp.int32)
            pl.semaphore_wait(barrier, peers)

        for k, (dr, dc) in enumerate(DIRECTIONS):

            if dr == 0 or dc == 0:

                @pl.when(exists(dr, dc))
                def _():
                    halo_copy(i, k).start()

            @pl.when(jnp.logical_not(exists(dr, dc)))
            def _():
                r0, rn = rows_in[dr]
                c0, cn = cols_in[dc]
                ext[i, :, r0 : r0 + rn, c0 : c0 + cn] = jnp.zeros((2, rn, cn), BF16)

    def one_hot(shape, shifted_axis, shift):
        along = lax.broadcasted_iota(jnp.int32, shape, shifted_axis)
        other = lax.broadcasted_iota(jnp.int32, shape, 1 - shifted_axis)
        return jnp.where(along == other + shift, F32(1), F32(0)).astype(BF16)

    for w in range(waves):
        r = pos_ref[0, 0, w] + RIM
        c = pos_ref[0, 1, w] + LANES
        span = slice(w * points, (w + 1) * points)
        cut_row[span, :] = one_hot((points, height), 1, r)
        cut_col[w] = one_hot((width, points), 0, c)
        put_row[:, span] = one_hot((height, points), 0, r)
        put_col[w] = one_hot((points, width), 1, c)

    f_left_h, f_left_l = dft_ref[0, 0], dft_ref[0, 1]
    f_right_h, f_right_l = dft_ref[1, 0], dft_ref[1, 1]
    f_full = f_right_h.astype(F32) + f_right_l.astype(F32)
    f_real, f_imag = f_full[:points, :points], f_full[:points, points:]

    def propagator(axis, sign):
        cosine, sine = cos_sin(prop_ref[axis : axis + 1, :])
        sine = sine * sign
        a_real = f_real * cosine + f_imag * sine
        a_imag = f_real * sine - f_imag * cosine
        return right_product(a_real, a_imag, f_right_h, f_right_l)

    def keep(n, top_right, bottom_left, real):
        high, low = split(
            jnp.concatenate(
                [
                    jnp.concatenate([real, top_right], axis=1),
                    jnp.concatenate([bottom_left, real], axis=1),
                ],
                axis=0,
            )
        )
        mats[n, 0] = high
        mats[n, 1] = low

    real, imag = propagator(0, 1.0)
    keep(0, -imag, imag, real)
    real, imag = propagator(1, -1.0)
    keep(1, -imag, imag, real)
    real, imag = propagator(0, -1.0)
    keep(2, -imag, imag, real)
    real, imag = propagator(1, 1.0)
    keep(3, -imag, imag, real)

    def patch_copy(i, k):
        mate = mates[k]
        return pltpu.make_async_remote_copy(
            src_ref=psend.at[mate, i],
            dst_ref=pat.at[d * group + i],
            send_sem=pat_s.at[i, k],
            recv_sem=pat_r.at[d * group + i],
            device_id={"depth": mate, "tile": t},
            device_id_type=MESH,
        )

    for i in range(group):
        for dr in (-1, 1):

            @pl.when(exists(dr, 0))
            def _():
                halo_arrival(i, DIRECTIONS.index((dr, 0))).wait_recv()
                for dc in (-1, 1):

                    @pl.when(exists(0, dc))
                    def _():
                        halo_copy(i, DIRECTIONS.index((dr, dc))).start()

        for k, (dr, dc) in enumerate(DIRECTIONS):
            if dc != 0:

                @pl.when(exists(dr, dc))
                def _():
                    halo_arrival(i, k).wait_recv()

        bands = [dot(cut_row[...], ext[i, c]).astype(BF16) for c in range(2)]
        for w in range(waves):
            span = slice(w * points, (w + 1) * points)
            both = jnp.concatenate([bands[0][span], bands[1][span]], axis=0)
            cut = dot(both, cut_col[w]).astype(BF16)
            psend[w, i, 0] = cut[:points]
            psend[w, i, 1] = cut[points:]
        for k in range(depth_count - 1):
            patch_copy(i, k).start()
        pat[d * group + i] = psend[d, i]

    def await_patch(s):
        @pl.when(s // group != d)
        def _():
            pltpu.make_async_remote_copy(
                src_ref=pat.at[s],
                dst_ref=pat.at[s],
                send_sem=pat_s.at[0, 0],
                recv_sem=pat_r.at[s],
                device_id={"depth": mates[0], "tile": t},
                device_id_type=MESH,
            ).wait_recv()

    def mixed(s):
        p_real, p_imag = pat[s, 0].astype(F32), pat[s, 1].astype(F32)
        w_real, w_imag = kept[s, 0], kept[s, 1]
        return p_real * w_real - p_imag * w_imag, p_real * w_imag + p_imag * w_real

    kept[0] = probe_ref[...]

    def forward(s, carry):
        await_patch(s)
        real, imag = mixed(s)
        real, imag = right_product(real, imag, mats[1, 0], mats[1, 1])
        real, imag = left_product(mats[0, 0], mats[0, 1], real, imag)
        kept[s + 1, 0] = real
        kept[s + 1, 1] = imag
        return carry

    lax.fori_loop(0, slices - 1, forward, 0)
    last = slices - 1
    await_patch(last)

    def contribution_copy(s):
        return pltpu.make_async_remote_copy(
            src_ref=csend.at[s],
            dst_ref=cin.at[s % group, d],
            send_sem=con_s.at[s],
            recv_sem=con_r.at[s % group, d],
            device_id={"depth": s // group, "tile": t},
            device_id_type=MESH,
        )

    def contribute(s, s_real, s_imag):
        w_real, w_imag = kept[s, 0], kept[s, 1]
        csend[s, 0] = (w_real * s_real + w_imag * s_imag).astype(BF16)
        csend[s, 1] = (w_real * s_imag - w_imag * s_real).astype(BF16)

        @pl.when(s // group != d)
        def _():
            contribution_copy(s).start()

        @pl.when(s // group == d)
        def _():
            cin[s % group, d] = csend[s]

        p_real, p_imag = pat[s, 0].astype(F32), pat[s, 1].astype(F32)
        back[0] = p_real * s_real + p_imag * s_imag
        back[1] = p_real * s_imag - p_imag * s_real

    real, imag = mixed(last)
    real, imag = right_product(real, imag, f_right_h, f_right_l)
    real, imag = left_product(f_left_h, f_left_l, real, imag)
    misfit = real * real + imag * imag - meas_ref[d]
    real, imag = right_product(misfit * real, misfit * imag, f_left_h, f_left_l)
    real, imag = left_product(f_right_h, f_right_l, real, imag)
    contribute(last, real, imag)

    def backward(number, carry):
        s = last - 1 - number
        real, imag = right_product(back[0], back[1], mats[3, 0], mats[3, 1])
        real, imag = left_product(mats[2, 0], mats[2, 1], real, imag)
        contribute(s, real, imag)
        return carry

    lax.fori_loop(0, slices - 1, backward, 0)

    def fold_copy(i, k):
        dr, dc = SIDES[k]
        back_k = SIDES.index((-dr, -dc))
        return pltpu.make_async_remote_copy(
            src_ref=rim_send[k].at[i],
            dst_ref=rim_recv[back_k].at[i],
            send_sem=fold_s.at[i, k],
            recv_sem=fold_r.at[i, back_k],
            device_id=neighbour(dr, dc),
            device_id_type=MESH,
        )

    def fold_arrival(i, k):
        dr, dc = SIDES[k]
        return pltpu.make_async_remote_copy(
            src_ref=rim_recv[k].at[i],
            dst_ref=rim_recv[k].at[i],
            send_sem=fold_s.at[i, k],
            recv_sem=fold_r.at[i, k],
            device_id=neighbour(dr, dc),
            device_id_type=MESH,
        )

    for i in reversed(range(group)):
        for w in range(waves):

            @pl.when(d != w)
            def _():
                pltpu.make_async_remote_copy(
                    src_ref=cin.at[i, w],
                    dst_ref=cin.at[i, w],
                    send_sem=con_s.at[0],
                    recv_sem=con_r.at[i, w],
                    device_id={"depth": mates[0], "tile": t},
                    device_id_type=MESH,
                ).wait_recv()

        for c in range(2):
            spread = [dot(cin[i, w, c], put_col[w]).astype(BF16) for w in range(waves)]
            grad[c] = dot(put_row[...], jnp.concatenate(spread, axis=0))
            for k, (dr, dc) in enumerate(SIDES[:2]):
                c0, cn = cols_in[dc]
                rim_send[k][i, c] = grad[c, :, c0 : c0 + cn].astype(BF16)
        for k, (dr, dc) in enumerate(SIDES[:2]):

            @pl.when(exists(dr, dc))
            def _():
                fold_copy(i, k).start()

        for k, (dr, dc) in enumerate(SIDES[:2]):

            @pl.when(exists(dr, dc))
            def _():
                fold_arrival(i, k).wait_recv()
                c0, cn = cols_own[dc]
                for c in range(2):
                    grad[c, :, c0 : c0 + cn] += rim_recv[k][i, c].astype(F32)

        for k, (dr, dc) in enumerate(SIDES):
            if dr:
                r0, rn = rows_in[dr]
                for c in range(2):
                    rim_send[k][i, c] = grad[c, r0 : r0 + rn, LANES : LANES + size].astype(BF16)

                @pl.when(exists(dr, dc))
                def _():
                    fold_copy(i, k).start()

        for c in range(2):
            out_ref[c, i, 0] = grad[c, RIM : RIM + size, LANES : LANES + size]

    for i in reversed(range(group)):
        for k, (dr, dc) in enumerate(SIDES):
            if dr:

                @pl.when(exists(dr, dc))
                def _():
                    fold_arrival(i, k).wait_recv()
                    r0 = 0 if dr < 0 else size - RIM
                    for c in range(2):
                        out_ref[c, i, 0, r0 : r0 + RIM, :] += rim_recv[k][i, c].astype(F32)

    for i in range(group):
        for k in range(depth_count - 1):
            patch_copy(i, k).wait_send()
        for k, (dr, dc) in enumerate(DIRECTIONS):

            @pl.when(exists(dr, dc))
            def _():
                halo_copy(i, k).wait_send()
                if k < len(SIDES):
                    fold_copy(i, SIDES.index((dr, dc))).wait_send()

    for s in range(slices):

        @pl.when(d != s // group)
        def _():
            contribution_copy(s).wait_send()


def shards(depth_count, tile_count, amplitude, phase_map, probe_wave, propagator_phase, positions, measured):
    columns = max(2, tile_count // 8)
    group, size = amplitude.shape[0], amplitude.shape[-1]
    points = probe_wave.shape[-1]
    waves = positions.shape[1]
    slices = group * depth_count
    assert waves == depth_count
    height, width = size + 2 * RIM, size + 2 * LANES
    rims = []
    for dr, dc in SIDES:
        shape = (group, 2, RIM if dr else height, size if dr else LANES)
        rims.append(pltpu.VMEM(shape, BF16))
    dma = pltpu.SemaphoreType.DMA
    vmem = pl.BlockSpec(memory_space=pltpu.VMEM)
    return pl.pallas_call(
        functools.partial(kernel, depth_count, tile_count, columns),
        out_shape=jax.ShapeDtypeStruct((2, group, 1, size, size), F32),
        in_specs=[pl.BlockSpec(memory_space=pltpu.SMEM)] + [vmem] * 6,
        out_specs=vmem,
        scratch_shapes=[
            pltpu.VMEM((group, 2, height, width), BF16),
            pltpu.VMEM((waves * points, height), BF16),
            pltpu.VMEM((waves, width, points), BF16),
            pltpu.VMEM((height, waves * points), BF16),
            pltpu.VMEM((waves, points, width), BF16),
            pltpu.VMEM((4, 2, 2 * points, 2 * points), BF16),
            pltpu.VMEM((waves, group, 2, points, points), BF16),
            pltpu.VMEM((slices, 2, points, points), BF16),
            pltpu.VMEM((slices, 2, points, points), F32),
            pltpu.VMEM((2, points, points), F32),
            pltpu.VMEM((slices, 2, points, points), BF16),
            pltpu.VMEM((group, waves, 2, points, points), BF16),
            pltpu.VMEM((2, height, width), F32),
            *rims,
            *rims,
            dma((group, 8)),
            dma((group, 8)),
            dma((group, depth_count)),
            dma((slices,)),
            dma((slices,)),
            dma((group, waves)),
            dma((group, 4)),
            dma((group, 4)),
        ],
        compiler_params=pltpu.CompilerParams(collective_id=0, has_side_effects=True),
    )(
        jnp.transpose(positions, (0, 2, 1)),
        amplitude,
        phase_map,
        probe_wave,
        propagator_phase,
        measured[0],
        jnp.asarray(dft_constants(points)),
    )


def solution(mesh):
    in_specs = (
        P("depth", "tile", None, None),
        P("depth", "tile", None, None),
        P(),
        P(),
        P("tile", None, None),
        P("tile", None, None, None),
    )
    out_specs = P(None, "depth", "tile", None, None)
    body = functools.partial(shards, mesh.shape["depth"], mesh.shape["tile"])
    return jax.shard_map(body, mesh=mesh, in_specs=in_specs, out_specs=out_specs, check_vma=False)
```

```python
import functools
import math

import jax
import jax.numpy as jnp
import numpy as np
from jax import lax
from jax.experimental import pallas as pl
from jax.experimental.pallas import tpu as pltpu
from jax.sharding import PartitionSpec as P

RIM = 64
LANES = 128
MESH = pl.DeviceIdType.MESH
F32 = jnp.float32
BF16 = jnp.bfloat16
SIDES = ((0, -1), (0, 1), (-1, 0), (1, 0))
DIRECTIONS = ((-1, 0), (1, 0), (0, -1), (0, 1)) + tuple((dr, dc) for dr in (-1, 1) for dc in (-1, 1))


def dft_constants(points):
    line = np.arange(points)
    angles = (line[:, None] * line[None, :] % points) * (-2.0 * math.pi / points)
    real = np.cos(angles) / math.sqrt(points)
    imag = np.sin(angles) / math.sqrt(points)
    left = np.block([[real, -imag], [imag, real]])
    right = np.block([[real, imag], [-imag, real]])
    both = np.stack([left, right]).astype(np.float32)
    high = both.astype(BF16)
    low = (both - high.astype(np.float32)).astype(BF16)
    return np.stack([high, low], axis=1)


def cos_sin(angle):
    half = angle * 0.5
    square = half * half
    sine = F32((1.0 / 6227020800.0))
    for term in (-1 / 39916800.0, 1 / 362880.0, -1 / 5040.0, 1 / 120.0, -1 / 6.0, 1.0):
        sine = sine * square + F32(term)
    sine = sine * half
    cosine = F32(1 / 479001600.0)
    for term in (-1 / 3628800.0, 1 / 40320.0, -1 / 720.0, 1 / 24.0, -0.5, 1.0):
        cosine = cosine * square + F32(term)
    return 1.0 - 2.0 * sine * sine, 2.0 * sine * cosine


def dot(a, b):
    return jnp.dot(a, b, preferred_element_type=F32)


def split(value):
    high = value.astype(BF16)
    return high, (value - high.astype(F32)).astype(BF16)


def right_product(real, imag, high, low):
    points = real.shape[-1]
    x_high, x_low = split(jnp.concatenate([real, imag], axis=1))
    result = dot(x_high, high) + (dot(x_low, high) + dot(x_high, low))
    return result[:, :points], result[:, points:]


def left_product(high, low, real, imag):
    points = real.shape[0]
    v_high, v_low = split(jnp.concatenate([real, imag], axis=0))
    both = dot(high, jnp.concatenate([v_high, v_low], axis=1))
    result = both[:, :points] + (both[:, points:] + dot(low, v_high))
    return result[:points], result[points:]


def kernel(
    depth_count,
    tile_count,
    columns,
    pos_ref,
    amp_ref,
    phase_ref,
    probe_ref,
    prop_ref,
    meas_ref,
    dft_ref,
    out_ref,
    ext,
    cut_row,
    cut_col,
    put_row,
    put_col,
    mats,
    psend,
    pat,
    kept,
    back,
    csend,
    cin,
    grad,
    spread,
    *rest,
):
    rim_send, rim_recv = rest[:4], rest[4:8]
    halo_s, halo_r, pat_s, pat_r, con_s, con_r, fold_s, fold_r = rest[8:]
    group, size = amp_ref.shape[0], amp_ref.shape[-1]
    waves, points = meas_ref.shape[0], meas_ref.shape[-1]
    slices = group * depth_count
    height = size + 2 * RIM
    width = size + 2 * LANES
    rows = tile_count // columns
    d = lax.axis_index("depth")
    t = lax.axis_index("tile")
    row, col = t // columns, t % columns

    def exists(dr, dc):
        return (row + dr >= 0) & (row + dr < rows) & (col + dc >= 0) & (col + dc < columns)

    def neighbour(dr, dc):
        return {"depth": d, "tile": t + dr * columns + dc}

    barrier = pltpu.get_barrier_semaphore()
    mates = [lax.rem(d + k, depth_count) for k in range(1, depth_count)]
    for mate in mates:
        pl.semaphore_signal(barrier, inc=1, device_id={"depth": mate, "tile": t}, device_id_type=MESH)
    for dr, dc in DIRECTIONS:

        @pl.when(exists(dr, dc))
        def _():
            pl.semaphore_signal(barrier, inc=1, device_id=neighbour(dr, dc), device_id_type=MESH)

    rows_in = {-1: (0, RIM), 0: (RIM, size), 1: (RIM + size, RIM)}
    cols_in = {-1: (0, LANES), 0: (LANES, size), 1: (LANES + size, LANES)}
    rows_own = {-1: (RIM, RIM), 0: (RIM, size), 1: (size, RIM)}
    cols_own = {-1: (LANES, LANES), 0: (LANES, size), 1: (size, LANES)}

    def halo_copy(i, k):
        dr, dc = DIRECTIONS[k]
        corner = dr != 0 and dc != 0
        far_row = dr if corner else -dr
        back_k = DIRECTIONS.index((far_row, -dc))
        return pltpu.make_async_remote_copy(
            src_ref=ext.at[i, :, pl.ds(*(rows_in if corner else rows_own)[dr]), pl.ds(*cols_own[dc])],
            dst_ref=ext.at[i, :, pl.ds(*rows_in[far_row]), pl.ds(*cols_in[-dc])],
            send_sem=halo_s.at[i, k],
            recv_sem=halo_r.at[i, back_k],
            device_id=neighbour(0 if corner else dr, dc),
            device_id_type=MESH,
        )

    def halo_arrival(i, k):
        dr, dc = DIRECTIONS[k]
        region = ext.at[i, :, pl.ds(*rows_in[dr]), pl.ds(*cols_in[dc])]
        return pltpu.make_async_remote_copy(
            src_ref=region,
            dst_ref=region,
            send_sem=halo_s.at[i, k],
            recv_sem=halo_r.at[i, k],
            device_id=neighbour(dr, dc),
            device_id_type=MESH,
        )

    for i in range(group):
        cosine, sine = cos_sin(phase_ref[i, 0])
        ext[i, 0, RIM : RIM + size, LANES : LANES + size] = (amp_ref[i, 0] * cosine).astype(BF16)
        ext[i, 1, RIM : RIM + size, LANES : LANES + size] = (amp_ref[i, 0] * sine).astype(BF16)
        if i == 0:
            peers = depth_count - 1
            for dr, dc in DIRECTIONS:
                peers += exists(dr, dc).astype(jnp.int32)
            pl.semaphore_wait(barrier, peers)

        for k, (dr, dc) in enumerate(DIRECTIONS):

            if dr == 0 or dc == 0:

                @pl.when(exists(dr, dc))
                def _():
                    halo_copy(i, k).start()

            @pl.when(jnp.logical_not(exists(dr, dc)))
            def _():
                r0, rn = rows_in[dr]
                c0, cn = cols_in[dc]
                ext[i, :, r0 : r0 + rn, c0 : c0 + cn] = jnp.zeros((2, rn, cn), BF16)

    def one_hot(shape, shifted_axis, shift):
        along = lax.broadcasted_iota(jnp.int32, shape, shifted_axis)
        other = lax.broadcasted_iota(jnp.int32, shape, 1 - shifted_axis)
        return jnp.where(along == other + shift, F32(1), F32(0)).astype(BF16)

    for w in range(waves):
        r = pos_ref[0, 0, w] + RIM
        c = pos_ref[0, 1, w] + LANES
        span = slice(w * points, (w + 1) * points)
        cut_row[span, :] = one_hot((points, height), 1, r)
        cut_col[w] = one_hot((width, points), 0, c)
        put_row[:, span] = one_hot((height, points), 0, r)
        put_col[w] = one_hot((points, width), 1, c)

    f_left_h, f_left_l = dft_ref[0, 0], dft_ref[0, 1]
    f_right_h, f_right_l = dft_ref[1, 0], dft_ref[1, 1]
    f_full = f_right_h.astype(F32) + f_right_l.astype(F32)
    f_real, f_imag = f_full[:points, :points], f_full[:points, points:]

    def propagator(axis, sign):
        cosine, sine = cos_sin(prop_ref[axis : axis + 1, :])
        sine = sine * sign
        a_real = f_real * cosine + f_imag * sine
        a_imag = f_real * sine - f_imag * cosine
        return right_product(a_real, a_imag, f_right_h, f_right_l)

    def keep(n, top_right, bottom_left, real):
        high, low = split(
            jnp.concatenate(
                [
                    jnp.concatenate([real, top_right], axis=1),
                    jnp.concatenate([bottom_left, real], axis=1),
                ],
                axis=0,
            )
        )
        mats[n, 0] = high
        mats[n, 1] = low

    real, imag = propagator(0, 1.0)
    keep(0, -imag, imag, real)
    real, imag = propagator(1, -1.0)
    keep(1, -imag, imag, real)
    real, imag = propagator(0, -1.0)
    keep(2, -imag, imag, real)
    real, imag = propagator(1, 1.0)
    keep(3, -imag, imag, real)

    def patch_copy(i, w):
        return pltpu.make_async_remote_copy(
            src_ref=psend.at[w, i],
            dst_ref=pat.at[d * group + i],
            send_sem=pat_s.at[i, w],
            recv_sem=pat_r.at[d * group + i],
            device_id={"depth": w, "tile": t},
            device_id_type=MESH,
        )

    for i in range(group):
        for dr in (-1, 1):

            @pl.when(exists(dr, 0))
            def _():
                halo_arrival(i, DIRECTIONS.index((dr, 0))).wait_recv()
                for dc in (-1, 1):

                    @pl.when(exists(0, dc))
                    def _():
                        halo_copy(i, DIRECTIONS.index((dr, dc))).start()

        for k, (dr, dc) in enumerate(DIRECTIONS):
            if dc != 0:

                @pl.when(exists(dr, dc))
                def _():
                    halo_arrival(i, k).wait_recv()

        for w in reversed(range(waves)):
            span = slice(w * points, (w + 1) * points)
            bands = [dot(cut_row[span], ext[i, c]).astype(BF16) for c in range(2)]
            cut = dot(jnp.concatenate(bands, axis=0), cut_col[w]).astype(BF16)
            psend[w, i, 0] = cut[:points]
            psend[w, i, 1] = cut[points:]

            @pl.when(d != w)
            def _():
                patch_copy(i, w).start()

        pat[d * group + i] = psend[d, i]

    def await_patch(s):
        @pl.when(s // group != d)
        def _():
            pltpu.make_async_remote_copy(
                src_ref=pat.at[s],
                dst_ref=pat.at[s],
                send_sem=pat_s.at[0, 0],
                recv_sem=pat_r.at[s],
                device_id={"depth": mates[0], "tile": t},
                device_id_type=MESH,
            ).wait_recv()

    def mixed(s):
        p_real, p_imag = pat[s, 0].astype(F32), pat[s, 1].astype(F32)
        w_real, w_imag = kept[s, 0], kept[s, 1]
        return p_real * w_real - p_imag * w_imag, p_real * w_imag + p_imag * w_real

    kept[0] = probe_ref[...]

    def forward(s, carry):
        await_patch(s)
        real, imag = mixed(s)
        real, imag = right_product(real, imag, mats[1, 0], mats[1, 1])
        real, imag = left_product(mats[0, 0], mats[0, 1], real, imag)
        kept[s + 1, 0] = real
        kept[s + 1, 1] = imag
        return carry

    lax.fori_loop(0, slices - 1, forward, 0)
    last = slices - 1
    await_patch(last)

    def contribution_copy(s):
        return pltpu.make_async_remote_copy(
            src_ref=csend.at[s],
            dst_ref=cin.at[s % group, d],
            send_sem=con_s.at[s],
            recv_sem=con_r.at[s % group, d],
            device_id={"depth": s // group, "tile": t},
            device_id_type=MESH,
        )

    def contribute(s, s_real, s_imag):
        w_real, w_imag = kept[s, 0], kept[s, 1]
        csend[s, 0] = (w_real * s_real + w_imag * s_imag).astype(BF16)
        csend[s, 1] = (w_real * s_imag - w_imag * s_real).astype(BF16)

        @pl.when(s // group != d)
        def _():
            contribution_copy(s).start()

        @pl.when(s // group == d)
        def _():
            cin[s % group, d] = csend[s]

        p_real, p_imag = pat[s, 0].astype(F32), pat[s, 1].astype(F32)
        back[0] = p_real * s_real + p_imag * s_imag
        back[1] = p_real * s_imag - p_imag * s_real

    real, imag = mixed(last)
    real, imag = right_product(real, imag, f_right_h, f_right_l)
    real, imag = left_product(f_left_h, f_left_l, real, imag)
    misfit = real * real + imag * imag - meas_ref[d]
    real, imag = right_product(misfit * real, misfit * imag, f_left_h, f_left_l)
    real, imag = left_product(f_right_h, f_right_l, real, imag)
    contribute(last, real, imag)

    def backward(number, carry):
        s = last - 1 - number
        real, imag = right_product(back[0], back[1], mats[3, 0], mats[3, 1])
        real, imag = left_product(mats[2, 0], mats[2, 1], real, imag)
        contribute(s, real, imag)
        return carry

    lax.fori_loop(0, slices - 1, backward, 0)

    def fold_copy(i, k):
        dr, dc = SIDES[k]
        back_k = SIDES.index((-dr, -dc))
        return pltpu.make_async_remote_copy(
            src_ref=rim_send[k].at[i],
            dst_ref=rim_recv[back_k].at[i],
            send_sem=fold_s.at[i, k],
            recv_sem=fold_r.at[i, back_k],
            device_id=neighbour(dr, dc),
            device_id_type=MESH,
        )

    def fold_arrival(i, k):
        dr, dc = SIDES[k]
        return pltpu.make_async_remote_copy(
            src_ref=rim_recv[k].at[i],
            dst_ref=rim_recv[k].at[i],
            send_sem=fold_s.at[i, k],
            recv_sem=fold_r.at[i, k],
            device_id=neighbour(dr, dc),
            device_id_type=MESH,
        )

    for i in reversed(range(group)):
        for w in range(waves):

            @pl.when(d != w)
            def _():
                pltpu.make_async_remote_copy(
                    src_ref=cin.at[i, w],
                    dst_ref=cin.at[i, w],
                    send_sem=con_s.at[0],
                    recv_sem=con_r.at[i, w],
                    device_id={"depth": mates[0], "tile": t},
                    device_id_type=MESH,
                ).wait_recv()

            for c in range(2):
                span = slice(w * points, (w + 1) * points)
                spread[c, span, :] = dot(cin[i, w, c], put_col[w]).astype(BF16)

        for k, (dr, dc) in enumerate(SIDES[:2]):
            c0, cn = cols_in[dc]
            for c in range(2):
                rim_send[k][i, c] = dot(put_row[...], spread[c, :, c0 : c0 + cn]).astype(BF16)
        for k, (dr, dc) in enumerate(SIDES[:2]):

            @pl.when(exists(dr, dc))
            def _():
                fold_copy(i, k).start()

        for c in range(2):
            grad[c] = dot(put_row[...], spread[c, :, LANES : LANES + size])

        for k, (dr, dc) in enumerate(SIDES[:2]):

            @pl.when(exists(dr, dc))
            def _():
                fold_arrival(i, k).wait_recv()
                c0, cn = cols_own[dc]
                for c in range(2):
                    grad[c, :, c0 - LANES : c0 - LANES + cn] += rim_recv[k][i, c].astype(F32)

        for k, (dr, dc) in enumerate(SIDES):
            if dr:
                r0, rn = rows_in[dr]
                for c in range(2):
                    rim_send[k][i, c] = grad[c, r0 : r0 + rn].astype(BF16)

                @pl.when(exists(dr, dc))
                def _():
                    fold_copy(i, k).start()

        for c in range(2):
            out_ref[c, i, 0] = grad[c, RIM : RIM + size]

    for i in reversed(range(group)):
        for k, (dr, dc) in enumerate(SIDES):
            if dr:

                @pl.when(exists(dr, dc))
                def _():
                    fold_arrival(i, k).wait_recv()
                    r0 = 0 if dr < 0 else size - RIM
                    for c in range(2):
                        out_ref[c, i, 0, r0 : r0 + RIM, :] += rim_recv[k][i, c].astype(F32)

    for i in range(group):
        for w in range(waves):

            @pl.when(d != w)
            def _():
                patch_copy(i, w).wait_send()

        for k, (dr, dc) in enumerate(DIRECTIONS):

            @pl.when(exists(dr, dc))
            def _():
                halo_copy(i, k).wait_send()
                if k < len(SIDES):
                    fold_copy(i, SIDES.index((dr, dc))).wait_send()

    for s in range(slices):

        @pl.when(d != s // group)
        def _():
            contribution_copy(s).wait_send()


def shards(depth_count, tile_count, amplitude, phase_map, probe_wave, propagator_phase, positions, measured):
    columns = max(2, tile_count // 8)
    group, size = amplitude.shape[0], amplitude.shape[-1]
    points = probe_wave.shape[-1]
    waves = positions.shape[1]
    slices = group * depth_count
    assert waves == depth_count
    height, width = size + 2 * RIM, size + 2 * LANES
    rims = []
    for dr, dc in SIDES:
        shape = (group, 2, RIM if dr else height, size if dr else LANES)
        rims.append(pltpu.VMEM(shape, BF16))
    dma = pltpu.SemaphoreType.DMA
    vmem = pl.BlockSpec(memory_space=pltpu.VMEM)
    return pl.pallas_call(
        functools.partial(kernel, depth_count, tile_count, columns),
        out_shape=jax.ShapeDtypeStruct((2, group, 1, size, size), F32),
        in_specs=[pl.BlockSpec(memory_space=pltpu.SMEM)] + [vmem] * 6,
        out_specs=vmem,
        scratch_shapes=[
            pltpu.VMEM((group, 2, height, width), BF16),
            pltpu.VMEM((waves * points, height), BF16),
            pltpu.VMEM((waves, width, points), BF16),
            pltpu.VMEM((height, waves * points), BF16),
            pltpu.VMEM((waves, points, width), BF16),
            pltpu.VMEM((4, 2, 2 * points, 2 * points), BF16),
            pltpu.VMEM((waves, group, 2, points, points), BF16),
            pltpu.VMEM((slices, 2, points, points), BF16),
            pltpu.VMEM((slices, 2, points, points), F32),
            pltpu.VMEM((2, points, points), F32),
            pltpu.VMEM((slices, 2, points, points), BF16),
            pltpu.VMEM((group, waves, 2, points, points), BF16),
            pltpu.VMEM((2, height, size), F32),
            pltpu.VMEM((2, waves * points, width), BF16),
            *rims,
            *rims,
            dma((group, 8)),
            dma((group, 8)),
            dma((group, waves)),
            dma((slices,)),
            dma((slices,)),
            dma((group, waves)),
            dma((group, 4)),
            dma((group, 4)),
        ],
        compiler_params=pltpu.CompilerParams(collective_id=0, has_side_effects=True),
    )(
        jnp.transpose(positions, (0, 2, 1)),
        amplitude,
        phase_map,
        probe_wave,
        propagator_phase,
        measured[0],
        jnp.asarray(dft_constants(points)),
    )


def solution(mesh):
    in_specs = (
        P("depth", "tile", None, None),
        P("depth", "tile", None, None),
        P(),
        P(),
        P("tile", None, None),
        P("tile", None, None, None),
    )
    out_specs = P(None, "depth", "tile", None, None)
    body = functools.partial(shards, mesh.shape["depth"], mesh.shape["tile"])
    return jax.shard_map(body, mesh=mesh, in_specs=in_specs, out_specs=out_specs, check_vma=False)
```

```python
import functools
import math

import jax
import jax.numpy as jnp
import numpy as np
from jax import lax
from jax.experimental import pallas as pl
from jax.experimental.pallas import tpu as pltpu
from jax.sharding import PartitionSpec as P

RIM = 64
LANES = 128
MESH = pl.DeviceIdType.MESH
F32 = jnp.float32
BF16 = jnp.bfloat16
SIDES = ((0, -1), (0, 1), (-1, 0), (1, 0))
DIRECTIONS = ((-1, 0), (1, 0), (0, -1), (0, 1)) + tuple((dr, dc) for dr in (-1, 1) for dc in (-1, 1))


def dft_constants(points):
    line = np.arange(points)
    angles = (line[:, None] * line[None, :] % points) * (-2.0 * math.pi / points)
    real = np.cos(angles) / math.sqrt(points)
    imag = np.sin(angles) / math.sqrt(points)
    left = np.block([[real, -imag], [imag, real]])
    right = np.block([[real, imag], [-imag, real]])
    both = np.stack([left, right]).astype(np.float32)
    high = both.astype(BF16)
    low = (both - high.astype(np.float32)).astype(BF16)
    return np.stack([high, low], axis=1)


def cos_sin(angle):
    half = angle * 0.5
    square = half * half
    sine = F32((1.0 / 6227020800.0))
    for term in (-1 / 39916800.0, 1 / 362880.0, -1 / 5040.0, 1 / 120.0, -1 / 6.0, 1.0):
        sine = sine * square + F32(term)
    sine = sine * half
    cosine = F32(1 / 479001600.0)
    for term in (-1 / 3628800.0, 1 / 40320.0, -1 / 720.0, 1 / 24.0, -0.5, 1.0):
        cosine = cosine * square + F32(term)
    return 1.0 - 2.0 * sine * sine, 2.0 * sine * cosine


def dot(a, b):
    return jnp.dot(a, b, preferred_element_type=F32)


def split(value):
    high = value.astype(BF16)
    return high, (value - high.astype(F32)).astype(BF16)


def right_product(real, imag, high, low):
    points = real.shape[-1]
    x_high, x_low = split(jnp.concatenate([real, imag], axis=1))
    result = dot(x_high, high) + (dot(x_low, high) + dot(x_high, low))
    return result[:, :points], result[:, points:]


def left_product(high, low, real, imag):
    points = real.shape[0]
    v_high, v_low = split(jnp.concatenate([real, imag], axis=0))
    both = dot(high, jnp.concatenate([v_high, v_low], axis=1))
    result = both[:, :points] + (both[:, points:] + dot(low, v_high))
    return result[:points], result[points:]


def kernel(
    depth_count,
    tile_count,
    columns,
    pos_ref,
    amp_ref,
    phase_ref,
    probe_ref,
    prop_ref,
    meas_ref,
    dft_ref,
    out_ref,
    ext,
    cut_row,
    cut_col,
    put_row,
    put_col,
    mats,
    psend,
    pat,
    kept,
    back,
    csend,
    cin,
    grad,
    *rest,
):
    rim_send, rim_recv = rest[:4], rest[4:8]
    halo_s, halo_r, pat_s, pat_r, con_s, con_r, fold_s, fold_r = rest[8:]
    group, size = amp_ref.shape[0], amp_ref.shape[-1]
    waves, points = meas_ref.shape[0], meas_ref.shape[-1]
    slices = group * depth_count
    height = size + 2 * RIM
    width = size + 2 * LANES
    rows = tile_count // columns
    d = lax.axis_index("depth")
    t = lax.axis_index("tile")
    row, col = t // columns, t % columns

    def exists(dr, dc):
        return (row + dr >= 0) & (row + dr < rows) & (col + dc >= 0) & (col + dc < columns)

    def neighbour(dr, dc):
        return {"depth": d, "tile": t + dr * columns + dc}

    barrier = pltpu.get_barrier_semaphore()
    mates = [lax.rem(d + k, depth_count) for k in range(1, depth_count)]
    for mate in mates:
        pl.semaphore_signal(barrier, inc=1, device_id={"depth": mate, "tile": t}, device_id_type=MESH)
    for dr, dc in DIRECTIONS:

        @pl.when(exists(dr, dc))
        def _():
            pl.semaphore_signal(barrier, inc=1, device_id=neighbour(dr, dc), device_id_type=MESH)

    rows_in = {-1: (0, RIM), 0: (RIM, size), 1: (RIM + size, RIM)}
    cols_in = {-1: (0, LANES), 0: (LANES, size), 1: (LANES + size, LANES)}
    rows_own = {-1: (RIM, RIM), 0: (RIM, size), 1: (size, RIM)}
    cols_own = {-1: (LANES, LANES), 0: (LANES, size), 1: (size, LANES)}

    def halo_copy(i, k):
        dr, dc = DIRECTIONS[k]
        corner = dr != 0 and dc != 0
        far_row = dr if corner else -dr
        back_k = DIRECTIONS.index((far_row, -dc))
        return pltpu.make_async_remote_copy(
            src_ref=ext.at[i, :, pl.ds(*(rows_in if corner else rows_own)[dr]), pl.ds(*cols_own[dc])],
            dst_ref=ext.at[i, :, pl.ds(*rows_in[far_row]), pl.ds(*cols_in[-dc])],
            send_sem=halo_s.at[i, k],
            recv_sem=halo_r.at[i, back_k],
            device_id=neighbour(0 if corner else dr, dc),
            device_id_type=MESH,
        )

    def halo_arrival(i, k):
        dr, dc = DIRECTIONS[k]
        region = ext.at[i, :, pl.ds(*rows_in[dr]), pl.ds(*cols_in[dc])]
        return pltpu.make_async_remote_copy(
            src_ref=region,
            dst_ref=region,
            send_sem=halo_s.at[i, k],
            recv_sem=halo_r.at[i, k],
            device_id=neighbour(dr, dc),
            device_id_type=MESH,
        )

    for i in range(group):
        cosine, sine = cos_sin(phase_ref[i, 0])
        ext[i, 0, RIM : RIM + size, LANES : LANES + size] = (amp_ref[i, 0] * cosine).astype(BF16)
        ext[i, 1, RIM : RIM + size, LANES : LANES + size] = (amp_ref[i, 0] * sine).astype(BF16)
        if i == 0:
            peers = depth_count - 1
            for dr, dc in DIRECTIONS:
                peers += exists(dr, dc).astype(jnp.int32)
            pl.semaphore_wait(barrier, peers)

        for k, (dr, dc) in enumerate(DIRECTIONS):

            if dr == 0 or dc == 0:

                @pl.when(exists(dr, dc))
                def _():
                    halo_copy(i, k).start()

            @pl.when(jnp.logical_not(exists(dr, dc)))
            def _():
                r0, rn = rows_in[dr]
                c0, cn = cols_in[dc]
                ext[i, :, r0 : r0 + rn, c0 : c0 + cn] = jnp.zeros((2, rn, cn), BF16)

    def one_hot(shape, shifted_axis, shift):
        along = lax.broadcasted_iota(jnp.int32, shape, shifted_axis)
        other = lax.broadcasted_iota(jnp.int32, shape, 1 - shifted_axis)
        return jnp.where(along == other + shift, F32(1), F32(0)).astype(BF16)

    for w in range(waves):
        r = pos_ref[0, 0, w] + RIM
        c = pos_ref[0, 1, w] + LANES
        span = slice(w * points, (w + 1) * points)
        cut_row[span, :] = one_hot((points, height), 1, r)
        cut_col[w] = one_hot((width, points), 0, c)
        put_row[:, span] = one_hot((height, points), 0, r)
        put_col[w] = one_hot((points, width), 1, c)

    f_left_h, f_left_l = dft_ref[0, 0], dft_ref[0, 1]
    f_right_h, f_right_l = dft_ref[1, 0], dft_ref[1, 1]
    f_full = f_right_h.astype(F32) + f_right_l.astype(F32)
    f_real, f_imag = f_full[:points, :points], f_full[:points, points:]

    def propagator(axis, sign):
        cosine, sine = cos_sin(prop_ref[axis : axis + 1, :])
        sine = sine * sign
        a_real = f_real * cosine + f_imag * sine
        a_imag = f_real * sine - f_imag * cosine
        return right_product(a_real, a_imag, f_right_h, f_right_l)

    def keep(n, top_right, bottom_left, real):
        high, low = split(
            jnp.concatenate(
                [
                    jnp.concatenate([real, top_right], axis=1),
                    jnp.concatenate([bottom_left, real], axis=1),
                ],
                axis=0,
            )
        )
        mats[n, 0] = high
        mats[n, 1] = low

    real, imag = propagator(0, 1.0)
    keep(0, -imag, imag, real)
    real, imag = propagator(1, -1.0)
    keep(1, -imag, imag, real)
    real, imag = propagator(0, -1.0)
    keep(2, -imag, imag, real)
    real, imag = propagator(1, 1.0)
    keep(3, -imag, imag, real)

    def patch_copy(i, k):
        mate = mates[k]
        return pltpu.make_async_remote_copy(
            src_ref=psend.at[mate, i],
            dst_ref=pat.at[d * group + i],
            send_sem=pat_s.at[i, k],
            recv_sem=pat_r.at[d * group + i],
            device_id={"depth": mate, "tile": t},
            device_id_type=MESH,
        )

    for i in range(group):
        for dr in (-1, 1):

            @pl.when(exists(dr, 0))
            def _():
                halo_arrival(i, DIRECTIONS.index((dr, 0))).wait_recv()
                for dc in (-1, 1):

                    @pl.when(exists(0, dc))
                    def _():
                        halo_copy(i, DIRECTIONS.index((dr, dc))).start()

        for k, (dr, dc) in enumerate(DIRECTIONS):
            if dc != 0:

                @pl.when(exists(dr, dc))
                def _():
                    halo_arrival(i, k).wait_recv()

        bands = [dot(cut_row[...], ext[i, c]).astype(BF16) for c in range(2)]
        for w in range(waves):
            span = slice(w * points, (w + 1) * points)
            both = jnp.concatenate([bands[0][span], bands[1][span]], axis=0)
            cut = dot(both, cut_col[w]).astype(BF16)
            psend[w, i, 0] = cut[:points]
            psend[w, i, 1] = cut[points:]
        for k in range(depth_count - 1):
            patch_copy(i, k).start()
        pat[d * group + i] = psend[d, i]

    def await_patch(s):
        @pl.when(s // group != d)
        def _():
            pltpu.make_async_remote_copy(
                src_ref=pat.at[s],
                dst_ref=pat.at[s],
                send_sem=pat_s.at[0, 0],
                recv_sem=pat_r.at[s],
                device_id={"depth": mates[0], "tile": t},
                device_id_type=MESH,
            ).wait_recv()

    def mixed(s):
        p_real, p_imag = pat[s, 0].astype(F32), pat[s, 1].astype(F32)
        w_real, w_imag = kept[s, 0], kept[s, 1]
        return p_real * w_real - p_imag * w_imag, p_real * w_imag + p_imag * w_real

    kept[0] = probe_ref[...]

    def forward(s, carry):
        await_patch(s)
        real, imag = mixed(s)
        real, imag = right_product(real, imag, mats[1, 0], mats[1, 1])
        real, imag = left_product(mats[0, 0], mats[0, 1], real, imag)
        kept[s + 1, 0] = real
        kept[s + 1, 1] = imag
        return carry

    lax.fori_loop(0, slices - 1, forward, 0)
    last = slices - 1
    await_patch(last)

    def contribution_copy(s):
        return pltpu.make_async_remote_copy(
            src_ref=csend.at[s],
            dst_ref=cin.at[s % group, d],
            send_sem=con_s.at[s],
            recv_sem=con_r.at[s % group, d],
            device_id={"depth": s // group, "tile": t},
            device_id_type=MESH,
        )

    def contribute(s, s_real, s_imag):
        w_real, w_imag = kept[s, 0], kept[s, 1]
        csend[s, 0] = (w_real * s_real + w_imag * s_imag).astype(BF16)
        csend[s, 1] = (w_real * s_imag - w_imag * s_real).astype(BF16)

        @pl.when(s // group != d)
        def _():
            contribution_copy(s).start()

        @pl.when(s // group == d)
        def _():
            cin[s % group, d] = csend[s]

        p_real, p_imag = pat[s, 0].astype(F32), pat[s, 1].astype(F32)
        back[0] = p_real * s_real + p_imag * s_imag
        back[1] = p_real * s_imag - p_imag * s_real

    real, imag = mixed(last)
    real, imag = right_product(real, imag, f_right_h, f_right_l)
    real, imag = left_product(f_left_h, f_left_l, real, imag)
    misfit = real * real + imag * imag - meas_ref[d]
    real, imag = right_product(misfit * real, misfit * imag, f_left_h, f_left_l)
    real, imag = left_product(f_right_h, f_right_l, real, imag)
    contribute(last, real, imag)

    def backward(number, carry):
        s = last - 1 - number
        real, imag = right_product(back[0], back[1], mats[3, 0], mats[3, 1])
        real, imag = left_product(mats[2, 0], mats[2, 1], real, imag)
        contribute(s, real, imag)
        return carry

    lax.fori_loop(0, slices - 1, backward, 0)

    def fold_copy(i, k):
        dr, dc = SIDES[k]
        back_k = SIDES.index((-dr, -dc))
        return pltpu.make_async_remote_copy(
            src_ref=rim_send[k].at[i],
            dst_ref=rim_recv[back_k].at[i],
            send_sem=fold_s.at[i, k],
            recv_sem=fold_r.at[i, back_k],
            device_id=neighbour(dr, dc),
            device_id_type=MESH,
        )

    def fold_arrival(i, k):
        dr, dc = SIDES[k]
        return pltpu.make_async_remote_copy(
            src_ref=rim_recv[k].at[i],
            dst_ref=rim_recv[k].at[i],
            send_sem=fold_s.at[i, k],
            recv_sem=fold_r.at[i, k],
            device_id=neighbour(dr, dc),
            device_id_type=MESH,
        )

    for i in reversed(range(group)):
        for w in range(waves):

            @pl.when(d != w)
            def _():
                pltpu.make_async_remote_copy(
                    src_ref=cin.at[i, w],
                    dst_ref=cin.at[i, w],
                    send_sem=con_s.at[0],
                    recv_sem=con_r.at[i, w],
                    device_id={"depth": mates[0], "tile": t},
                    device_id_type=MESH,
                ).wait_recv()

        for c in range(2):
            spread = [dot(cin[i, w, c], put_col[w]).astype(BF16) for w in range(waves)]
            grad[c] = dot(put_row[...], jnp.concatenate(spread, axis=0))
            for k, (dr, dc) in enumerate(SIDES[:2]):
                c0, cn = cols_in[dc]
                rim_send[k][i, c] = grad[c, :, c0 : c0 + cn].astype(BF16)
        for k, (dr, dc) in enumerate(SIDES[:2]):

            @pl.when(exists(dr, dc))
            def _():
                fold_copy(i, k).start()

        for k, (dr, dc) in enumerate(SIDES[:2]):

            @pl.when(exists(dr, dc))
            def _():
                fold_arrival(i, k).wait_recv()
                c0, cn = cols_own[dc]
                for c in range(2):
                    grad[c, :, c0 : c0 + cn] += rim_recv[k][i, c].astype(F32)

        for k, (dr, dc) in enumerate(SIDES):
            if dr:
                r0, rn = rows_in[dr]
                for c in range(2):
                    rim_send[k][i, c] = grad[c, r0 : r0 + rn, LANES : LANES + size].astype(BF16)

                @pl.when(exists(dr, dc))
                def _():
                    fold_copy(i, k).start()

        for c in range(2):
            out_ref[c, i, 0] = grad[c, RIM : RIM + size, LANES : LANES + size].astype(BF16)

    for i in reversed(range(group)):
        for k, (dr, dc) in enumerate(SIDES):
            if dr:

                @pl.when(exists(dr, dc))
                def _():
                    fold_arrival(i, k).wait_recv()
                    r0 = 0 if dr < 0 else size - RIM
                    for c in range(2):
                        held = out_ref[c, i, 0, r0 : r0 + RIM, :].astype(F32)
                        out_ref[c, i, 0, r0 : r0 + RIM, :] = (held + rim_recv[k][i, c].astype(F32)).astype(BF16)

    for i in range(group):
        for k in range(depth_count - 1):
            patch_copy(i, k).wait_send()
        for k, (dr, dc) in enumerate(DIRECTIONS):

            @pl.when(exists(dr, dc))
            def _():
                halo_copy(i, k).wait_send()
                if k < len(SIDES):
                    fold_copy(i, SIDES.index((dr, dc))).wait_send()

    for s in range(slices):

        @pl.when(d != s // group)
        def _():
            contribution_copy(s).wait_send()


def shards(depth_count, tile_count, amplitude, phase_map, probe_wave, propagator_phase, positions, measured):
    columns = max(2, tile_count // 8)
    group, size = amplitude.shape[0], amplitude.shape[-1]
    points = probe_wave.shape[-1]
    waves = positions.shape[1]
    slices = group * depth_count
    assert waves == depth_count
    height, width = size + 2 * RIM, size + 2 * LANES
    rims = []
    for dr, dc in SIDES:
        shape = (group, 2, RIM if dr else height, size if dr else LANES)
        rims.append(pltpu.VMEM(shape, BF16))
    dma = pltpu.SemaphoreType.DMA
    vmem = pl.BlockSpec(memory_space=pltpu.VMEM)
    return pl.pallas_call(
        functools.partial(kernel, depth_count, tile_count, columns),
        out_shape=jax.ShapeDtypeStruct((2, group, 1, size, size), BF16),
        in_specs=[pl.BlockSpec(memory_space=pltpu.SMEM)] + [vmem] * 6,
        out_specs=vmem,
        scratch_shapes=[
            pltpu.VMEM((group, 2, height, width), BF16),
            pltpu.VMEM((waves * points, height), BF16),
            pltpu.VMEM((waves, width, points), BF16),
            pltpu.VMEM((height, waves * points), BF16),
            pltpu.VMEM((waves, points, width), BF16),
            pltpu.VMEM((4, 2, 2 * points, 2 * points), BF16),
            pltpu.VMEM((waves, group, 2, points, points), BF16),
            pltpu.VMEM((slices, 2, points, points), BF16),
            pltpu.VMEM((slices, 2, points, points), F32),
            pltpu.VMEM((2, points, points), F32),
            pltpu.VMEM((slices, 2, points, points), BF16),
            pltpu.VMEM((group, waves, 2, points, points), BF16),
            pltpu.VMEM((2, height, width), F32),
            *rims,
            *rims,
            dma((group, 8)),
            dma((group, 8)),
            dma((group, depth_count)),
            dma((slices,)),
            dma((slices,)),
            dma((group, waves)),
            dma((group, 4)),
            dma((group, 4)),
        ],
        compiler_params=pltpu.CompilerParams(collective_id=0, has_side_effects=True),
    )(
        jnp.transpose(positions, (0, 2, 1)),
        amplitude,
        phase_map,
        probe_wave,
        propagator_phase,
        measured[0],
        jnp.asarray(dft_constants(points)),
    ).astype(F32)


def solution(mesh):
    in_specs = (
        P("depth", "tile", None, None),
        P("depth", "tile", None, None),
        P(),
        P(),
        P("tile", None, None),
        P("tile", None, None, None),
    )
    out_specs = P(None, "depth", "tile", None, None)
    body = functools.partial(shards, mesh.shape["depth"], mesh.shape["tile"])
    return jax.shard_map(body, mesh=mesh, in_specs=in_specs, out_specs=out_specs, check_vma=False)
```
